32 devices in a mesh: prow: 8 (over z, y), pcol: 4 (over x, core).
Axes of the slice: x: 2, y: 2, z: 4, core: 2. Of those that a mesh axis runs over, the one named last changes fastest.
Arguments:
- paper_x: bfloat16 [8192, 768], P(('prow', 'pcol')), may hold values from -6 to 6
- author_x: bfloat16 [4096, 768], P(('pcol', 'prow')), may hold values from -6 to 6
- w_self: bfloat16 [768, 768], replicated, may hold values from -0.21875 to 0.21875
- w_rel: bfloat16 [2, 768, 768], replicated, may hold values from -0.009765625 to 0.009765625
- w_two: bfloat16 [768, 768], replicated, may hold values from -0.0068359375 to 0.0068359375
- block_rows: int32 [8, 4, 32], P('prow', 'pcol'), may hold values from 0 to 7, as said below
- block_cols: int32 [8, 4, 32], P('prow', 'pcol'), may hold values from 0 to 7, as said below
- block_type: int32 [8, 4, 32], P('prow', 'pcol'), may hold values from 0 to 1
- block_count: int32 [8, 4], P('prow', 'pcol'), may hold values from 8 to 32, as said below
- block_vals: bfloat16 [8, 4, 32, 128, 128], P('prow', 'pcol'), may hold values from 0 to 1, as said below
Outputs:
- paper_hidden: bfloat16 [8192, 768], P(('prow', 'pcol'))
- author_out: bfloat16 [4096, 768], P(('pcol', 'prow'))
The draws below stay inside these ranges and needn't reach their ends.
Inputs may be any that keep to these rules, and one draw needn't show every extreme that they name: `block_rows`: within one tile the live and dead slots name distinct positions; block rows are below 8. `block_cols`: block columns are below 8; with block_rows, positions of one tile are distinct. `block_count`: slots 0 to count - 1 of a tile are live; some tile holds 32 live slots and some tile 32 // 4 in every draw. `block_vals`: every entry is 0 or 1.
All inputs are finite; a program needn't handle non-finite values.
Results may differ from the reference program's by a relative error of at most 0.0041.
Values may be sent and summed in bfloat16 or wider, within the bound.
A program may use at most 64 MiB of HBM per device.

```python
import jax
import jax.numpy as jnp
from jax import lax

WIDTH = 768
BLOCK = 128
RELATIONS = 2
ROW_BLOCKS = 8
COL_BLOCKS = 8
SLOTS = 32
PAPERS = 8192
AUTHORS = 4096
N_PROW = 8
N_PCOL = 4


def tile_positions(key):
    keys = jax.random.split(jax.random.fold_in(key, 7), N_PROW * N_PCOL)
    chosen = jax.vmap(lambda single: jax.random.permutation(single, ROW_BLOCKS * COL_BLOCKS)[:SLOTS])(keys)
    return chosen.reshape(N_PROW, N_PCOL, SLOTS).astype(jnp.int32)


def draw_block_rows(key, part):
    return (tile_positions(key) // COL_BLOCKS).astype(jnp.int32)


def draw_block_cols(key, part):
    return (tile_positions(key) % COL_BLOCKS).astype(jnp.int32)


def draw_block_count(key, part):
    tiles = N_PROW * N_PCOL
    counts = jax.random.randint(jax.random.fold_in(key, 11), (tiles,), SLOTS // 4, SLOTS + 1)
    fullest = jax.random.randint(jax.random.fold_in(key, 12), (), 0, tiles)
    offset = jax.random.randint(jax.random.fold_in(key, 13), (), 0, tiles - 1)
    emptiest = (fullest + 1 + offset) % tiles
    places = jnp.arange(tiles, dtype=jnp.int32)
    counts = jnp.where(places == fullest, SLOTS, counts)
    counts = jnp.where(places == emptiest, SLOTS // 4, counts)
    return counts.reshape(N_PROW, N_PCOL).astype(jnp.int32)


def draw_block_vals(key, part):
    shape = (N_PROW, N_PCOL, SLOTS, BLOCK, BLOCK)
    ones = jax.random.bernoulli(jax.random.fold_in(key, 17), 0.5, shape).astype(jnp.float32)
    return ones.astype(jnp.bfloat16)


def with_ends(array, rng, least, largest):
    index_at = [jax.random.randint(jax.random.fold_in(rng, axis), (), 0, length) for axis, length in enumerate(array.shape)]
    main_axis = array.shape.index(max(array.shape))
    next_to = index_at[:main_axis] + [(index_at[main_axis] + 1) % array.shape[main_axis]] + index_at[main_axis + 1:]
    return array.at[tuple(index_at)].set(least).at[tuple(next_to)].set(largest)


def shard_levels(rng, dims, cuts, least, high):
    level = 1.0
    for position, shards_of in cuts:
        steps = jax.random.uniform(jax.random.fold_in(jax.random.fold_in(rng, 6), position), (shards_of,), jnp.float32, least / len(cuts), high / len(cuts))
        level = level * jnp.repeat(jnp.exp(steps), dims[position] // shards_of).reshape((-1,) + (1,) * (len(dims) - 1 - position))
    return level


def scatter_about(key, dims, width, most, cuts=(), kind=jnp.bfloat16):
    array = jax.random.normal(key, dims, jnp.float32) * width
    if len(cuts) > 0:
        array = shard_levels(key, dims, cuts, -0.22, 0.18) * array
    return jnp.clip(array, min=-most, max=most).astype(kind)


def setup_inputs(seed: int = 0) -> dict:
    arg_keys = jax.random.split(jax.random.key(seed), 11)
    return {
        "paper_x": scatter_about(arg_keys[0], (PAPERS, WIDTH), 1.0, 6.0, ((0, 32),)),
        "author_x": scatter_about(arg_keys[1], (AUTHORS, WIDTH), 1.0, 6.0, ((0, 32),)),
        "w_self": scatter_about(arg_keys[2], (WIDTH, WIDTH), WIDTH ** -0.5, 0.21875),
        "w_rel": scatter_about(arg_keys[3], (RELATIONS, WIDTH, WIDTH), (WIDTH * (BLOCK // 4) * SLOTS * N_PCOL // ROW_BLOCKS) ** -0.5, 0.009765625),
        "w_two": scatter_about(arg_keys[4], (WIDTH, WIDTH), (WIDTH * (BLOCK // 4) * SLOTS * N_PROW // COL_BLOCKS) ** -0.5, 0.0068359375),
        "block_rows": draw_block_rows(jax.random.fold_in(arg_keys[10], 71), 0),
        "block_cols": draw_block_cols(jax.random.fold_in(arg_keys[10], 71), 0),
        "block_type": with_ends(jax.random.randint(arg_keys[7], (N_PROW, N_PCOL, SLOTS), 0, RELATIONS), jax.random.fold_in(arg_keys[7], 1), 0, RELATIONS - 1).astype(jnp.int32),
        "block_count": draw_block_count(jax.random.fold_in(arg_keys[10], 71), 0),
        "block_vals": draw_block_vals(jax.random.fold_in(arg_keys[10], 71), 0),
    }


def reference(paper_x, author_x, w_self, w_rel, w_two, block_rows, block_cols, block_type, block_count, block_vals):
    paper_blocks = PAPERS // BLOCK
    author_blocks = AUTHORS // BLOCK
    tiles = N_PROW * N_PCOL
    messages = jnp.stack([jnp.dot(author_x, w_rel[index], preferred_element_type=jnp.float32) for index in range(RELATIONS)]).astype(jnp.bfloat16)
    grid_row = (jnp.arange(N_PROW, dtype=jnp.int32)[:, None, None] * ROW_BLOCKS + block_rows).reshape(tiles, SLOTS).astype(jnp.int32)
    grid_col = (jnp.arange(N_PCOL, dtype=jnp.int32)[None, :, None] * COL_BLOCKS + block_cols).reshape(tiles, SLOTS).astype(jnp.int32)
    type_ids = block_type.reshape(tiles, SLOTS)
    live = (jnp.arange(SLOTS, dtype=jnp.int32)[None, None, :] < block_count[:, :, None]).astype(jnp.float32).reshape(tiles, SLOTS)
    contents = block_vals.reshape(tiles, SLOTS, BLOCK, BLOCK)
    table = messages.reshape(RELATIONS * author_blocks, BLOCK, WIDTH)

    def first_hop(total, item):
        rows_now, cols_now, types_now, mask_now, content_now = item
        picked = table[(types_now * author_blocks + cols_now).astype(jnp.int32)]
        product = jnp.einsum("kpa,kaf->kpf", content_now.astype(jnp.float32), picked.astype(jnp.float32))
        return total.at[rows_now].add(product * mask_now[:, None, None]), None

    start = jnp.zeros((paper_blocks, BLOCK, WIDTH), jnp.float32)
    gathered, _ = lax.scan(first_hop, start, (grid_row, grid_col, type_ids, live, contents))
    gathered = gathered.reshape(PAPERS, WIDTH)
    self_term = jnp.dot(paper_x, w_self, preferred_element_type=jnp.float32)
    paper_hidden = jnp.maximum(self_term + gathered, 0.0).astype(jnp.bfloat16)
    outgoing = jnp.dot(paper_hidden, w_two, preferred_element_type=jnp.float32).astype(jnp.bfloat16)
    paper_table = outgoing.reshape(paper_blocks, BLOCK, WIDTH)

    def second_hop(total, item):
        rows_now, cols_now, mask_now, content_now = item
        picked = paper_table[rows_now]
        product = jnp.einsum("kpa,kpf->kaf", content_now.astype(jnp.float32), picked.astype(jnp.float32))
        return total.at[cols_now].add(product * mask_now[:, None, None]), None

    start_two = jnp.zeros((author_blocks, BLOCK, WIDTH), jnp.float32)
    author_total, _ = lax.scan(second_hop, start_two, (grid_row, grid_col, live, contents))
    author_out = author_total.reshape(AUTHORS, WIDTH).astype(jnp.bfloat16)
    return paper_hidden, author_out
```

```python
import functools

import jax
import jax.numpy as jnp
from jax import lax
from jax.experimental import pallas as pl
from jax.experimental.pallas import tpu as pltpu
from jax.sharding import PartitionSpec as P

MESH = pl.DeviceIdType.MESH
F32 = jnp.float32
BF16 = jnp.bfloat16


def dot(a, b):
    return jnp.dot(a, b, preferred_element_type=F32)


def kernel(
    n_prow, n_pcol, wide, fc,
    tab, author_h, paper_h, w_self_h, w_rel_h, w_two_h, blocks_h,
    hidden_h, author_out,
    paper, w_self, w_rel, w_two, blocks,
    x_all, msgs, dense, dense_t, acc,
    pair_out, pair_in, x_out, x_in, h_all, hidden,
    y_out, y_in, y_acc, z_out, z_in, out_acc,
    local_sem,
    g_send, g_recv, gy_send, gy_recv,
    pair_s, pair_r, xs, xr, hs, hr,
    ys, yr, zs, zr,
):
    i = lax.axis_index("prow")
    j = lax.axis_index("pcol")
    z, y = i // 2, i % 2
    x, c = j // 2, j % 2
    H, G = n_prow // 2, n_pcol // 2
    own_papers, width = paper.shape
    own_authors = author_h.shape[0]
    side = blocks.shape[1]
    authors = own_authors * n_prow
    papers = own_papers * n_pcol
    pair_authors = 2 * own_authors
    nf, nb = width // fc, width // wide
    per = wide // fc
    y_part = z * 2 + 1 - y
    c_part = x * 2 + 1 - c
    low = z < H // 2

    waits = []

    def send(cond, src, dst, ss, rs, di, dj):
        def desc():
            return pltpu.make_async_remote_copy(
                src_ref=src, dst_ref=dst, send_sem=ss, recv_sem=rs,
                device_id=(di, dj), device_id_type=MESH,
            )

        if cond is None:
            desc().start()
        else:
            @pl.when(cond)
            def _():
                desc().start()
        waits.append((cond, desc))

    def arrive(dst, ss, rs):
        pltpu.make_async_remote_copy(
            src_ref=dst, dst_ref=dst, send_sem=ss, recv_sem=rs,
            device_id=(i, c_part), device_id_type=MESH,
        ).wait_recv()

    barrier = pltpu.get_barrier_semaphore()

    def greet(cond, di, dj):
        def go():
            pl.semaphore_signal(barrier, inc=1, device_id=(di, dj), device_id_type=MESH)

        if cond is None:
            go()
        else:
            pl.when(cond)(go)

    up_z, down_z = z < H - 1, z > 0
    greet(up_z, i + 2, j)
    greet(down_z, i - 2, j)
    greet(None, y_part, j)
    for d in range(1, G):
        greet(None, i, lax.rem(x + d, G) * 2 + c)
    greet(None, i, c_part)
    for d in range(2, H):
        greet(z + d <= H - 1, i + 2 * d, j)
        greet(z - d >= 0, i - 2 * d, j)

    loads = [
        pltpu.make_async_copy(src, dst, local_sem.at[n])
        for n, (src, dst) in enumerate(
            (
                (blocks_h, blocks), (w_rel_h, w_rel), (paper_h, paper), (w_self_h, w_self), (w_two_h, w_two),
                (author_h, x_all.at[z, y]),
            )
        )
    ]
    for load in loads:
        load.start()

    pl.semaphore_wait(barrier, 1 + G + H - 1)

    parts = g_send.shape[2]
    part_rows = own_authors // parts

    def piece(zz, yy, h):
        return x_all.at[zz, yy, pl.ds(h * part_rows, part_rows), :]

    for h in range(parts):
        mine = author_h.at[pl.ds(h * part_rows, part_rows), :]
        send(up_z, mine, piece(z, y, h), g_send.at[0, 0, h], g_recv.at[0, 0, h], i + 2, j)
        send(down_z, mine, piece(z, y, h), g_send.at[1, 0, h], g_recv.at[1, 0, h], i - 2, j)
        send(None, mine, piece(z, y, h), gy_send.at[2, 0, h], gy_recv.at[2, 0, h], y_part, j)

    loads[0].wait()
    row_blocks, col_blocks = papers // side, authors // side
    p_step, a_step, pair_step = min(side, own_papers), min(side, own_authors), min(side, pair_authors)

    def densify(first, last):
        for rb in range(first, last):
            for cb in range(col_blocks):
                pos = rb * col_blocks + cb
                slot, kind = tab[0, pos], tab[1, pos]
                block = blocks[slot].astype(F32)
                for t in range(2):
                    part = (block * (kind == t).astype(F32)).astype(BF16)
                    for sub in range(side // p_step):
                        row = rb * side + sub * p_step
                        for lane in range(side // pair_step):
                            col = cb * side + lane * pair_step
                            lo = t * pair_authors + col % pair_authors
                            dense[
                                col // pair_authors, row // own_papers,
                                row % own_papers:row % own_papers + p_step, lo:lo + pair_step,
                            ] = part[sub * p_step:(sub + 1) * p_step, lane * pair_step:(lane + 1) * pair_step]
                flip = (block * (kind < 2).astype(F32)).T.astype(BF16)
                for sub in range(side // a_step):
                    owner = (cb * side + sub * a_step) // own_authors
                    dense_t[owner % 2, owner // 2, :, rb * side:(rb + 1) * side] = flip[sub * a_step:(sub + 1) * a_step]

    def z_arrival(s):
        for h in range(parts):
            for way, near, inside, more, to in (
                (0, z - 1 - s, z - 1 - s >= 0, up_z, i + 2),
                (1, z + 1 + s, z + 1 + s <= H - 1, down_z, i - 2),
            ):
                part = piece(near, y, h)

                @pl.when(inside)
                def _():
                    arrive(part, g_send.at[way, s, h], g_recv.at[way, s, h])

                if s + 1 <= H - 2:
                    send(inside & more, part, part, g_send.at[way, s + 1, h], g_recv.at[way, s + 1, h], to, j)
                send(inside, part, part, gy_send.at[way, s, h], gy_recv.at[way, s, h], y_part, j)

    def messages(zz, n):
        pair = x_all[zz].reshape(pair_authors, width)
        cols = slice(n * wide, (n + 1) * wide)
        for t in range(2):
            msgs[zz, t * pair_authors:(t + 1) * pair_authors, cols] = dot(pair, w_rel[t, :, cols]).astype(BF16)

    def hop_one(zz, n, b, cc, first):
        part = dot(dense[zz, b * 2 + cc], msgs[zz, :, n * wide:(n + 1) * wide])
        for p in range(per):
            value = part[:, p * fc:(p + 1) * fc]
            f = n * per + p
            acc[f, b, cc] = value if first else acc[f, b, cc] + value

    def slab(zz, first):
        for n in range(nb):
            messages(zz, n)
            for b in range(G):
                for cc in range(2):
                    hop_one(zz, n, b, cc, first)

    reach = jnp.minimum(z, H - 1 - z)

    def order(k):
        both = k < 2 * reach
        dist = jnp.where(both, k // 2 + 1, k - reach + 1)
        above = jnp.where(both, k % 2 == 0, low)
        return dist, above.astype(jnp.int32), jnp.where(above, z + dist, z - dist)

    def from_y(k):
        dist, way, near = order(k)
        for h in range(parts):
            arrive(piece(near, 1 - y, h), gy_send.at[way, dist - 1, h], gy_recv.at[way, dist - 1, h])
        return near

    half = row_blocks // 2
    densify(0, half)
    z_arrival(0)
    densify(half, row_blocks)
    for load in loads[1:]:
        load.wait()
    for h in range(parts):
        arrive(piece(z, 1 - y, h), gy_send.at[2, 0, h], gy_recv.at[2, 0, h])
    slab(z, True)
    for n in range(nb):
        cols = slice(n * wide, (n + 1) * wide)
        own = dot(paper[...], w_self[:, cols])
        for p in range(per):
            f = n * per + p
            acc[f, x, c] = acc[f, x, c] + own[:, p * fc:(p + 1) * fc]
    if H > 2:
        z_arrival(1)
    for k in range(H - 2):
        slab(from_y(k), False)
        if k + 2 <= H - 2:
            z_arrival(k + 2)
    last = from_y(H - 2)

    def to_pair(n):
        messages(last, n)
        for b in range(G):
            hop_one(last, n, b, 1 - c, False)
        for p in range(per):
            f = n * per + p
            for b in range(G):
                pair_out[f, b] = acc[f, b, 1 - c].astype(BF16)
            send(None, pair_out.at[f], pair_in.at[f], pair_s.at[f], pair_r.at[f], i, c_part)
        for b in range(G):
            hop_one(last, n, b, c, False)

    def to_x(f):
        arrive(pair_in.at[f], pair_s.at[f], pair_r.at[f])
        for b in range(G):
            total = acc[f, b, c] + pair_in[f, b].astype(F32)
            acc[f, b, c] = total
            x_out[f, b] = total.astype(BF16)
        for d in range(1, G):
            send(None, x_out.at[f], x_in.at[d - 1, f], xs.at[d - 1, f], xr.at[d - 1, f],
                 i, lax.rem(x + d, G) * 2 + c)

    def from_x(f):
        for d in range(1, G):
            arrive(x_in.at[d - 1, f], xs.at[d - 1, f], xr.at[d - 1, f])
        for b in range(G):
            total = acc[f, b, c]
            for d in range(1, G):
                total = total + x_in[d - 1, f, b].astype(F32)
            h_all[f, c, b] = jnp.maximum(total, 0.0).astype(BF16)
        send(None, h_all.at[f, c], h_all.at[f, c], hs.at[f], hr.at[f], i, c_part)
        hidden[:, f * fc:(f + 1) * fc] = h_all[f, c, x]

    def target(k):
        return jnp.where(low, H - 1 - k, k)

    def to_y(f):
        arrive(h_all.at[f, 1 - c], hs.at[f], hr.at[f])
        table = jnp.concatenate(
            [h_all[f, q % 2, q // 2] for q in range(n_pcol)], axis=0
        )
        far = dot(dense_t[1 - y].reshape(H * own_authors, papers), table)
        y_out[f] = far.astype(BF16).reshape(H, own_authors, fc)
        for k in range(H):
            b = target(k)
            send(None, y_out.at[f, b], y_in.at[f, b], ys.at[f, b], yr.at[f, b], y_part, j)
        near = dot(dense_t[y].reshape(H * own_authors, papers), table)
        y_acc[f] = near.reshape(H, own_authors, fc)

    def to_z(f):
        for k in range(H):
            b = target(k)
            arrive(y_in.at[f, b], ys.at[f, b], yr.at[f, b])
            total = y_acc[f, b] + y_in[f, b].astype(F32)
            y_acc[f, b] = total
            z_out[f, b] = total.astype(BF16)
            send(b != z, z_out.at[f, b], z_in.at[f, z], zs.at[f, b], zr.at[f, z], b * 2 + y, j)

    def finish(f):
        for s in range(H):
            @pl.when(z != s)
            def _():
                arrive(z_in.at[f, s], zs.at[f, s], zr.at[f, s])
                y_acc[f, z] = y_acc[f, z] + z_in[f, s].astype(F32)

        total = y_acc[f, z]
        high = total.astype(BF16)
        rest = (total - high.astype(F32)).astype(BF16)
        for n in range(nb):
            cols = slice(n * wide, (n + 1) * wide)
            weight = w_two[f * fc:(f + 1) * fc, cols]
            value = dot(high, weight) + dot(rest, weight)
            out_acc[:, cols] = value if f == 0 else out_acc[:, cols] + value

    for n in range(nb):
        to_pair(n)
        if n > 0:
            for p in range(per):
                to_x((n - 1) * per + p)
    for p in range(per):
        to_x((nb - 1) * per + p)

    for f in range(nf):
        from_x(f)
        to_y(f)
        if f >= 1:
            to_z(f - 1)
        if f >= 4:
            finish(f - 4)
    store = pltpu.make_async_copy(hidden, hidden_h, local_sem.at[0])
    store.start()
    for f in range(max(nf - 4, 0), nf - 2):
        finish(f)
    to_z(nf - 1)
    for f in range(max(nf - 2, 0), nf):
        finish(f)
    author_out[...] = out_acc[...].astype(BF16)
    store.wait()

    for cond, desc in waits:
        if cond is None:
            desc().wait_send()
        else:
            @pl.when(cond)
            def _():
                desc().wait_send()


def per_device(
    n_prow, n_pcol, paper_x, author_x, w_self, w_rel, w_two,
    block_rows, block_cols, block_type, block_count, block_vals,
):
    slots, side = block_vals.shape[2], block_vals.shape[3]
    own_papers, width = paper_x.shape
    own_authors = author_x.shape[0]
    papers, authors = own_papers * n_pcol, own_authors * n_prow
    col_blocks = authors // side
    places = (papers // side) * col_blocks
    H, G = n_prow // 2, n_pcol // 2
    wide = 256 if width % 256 == 0 else 128
    fc = 128
    nf = width // fc

    slot = jnp.arange(slots, dtype=jnp.int32)
    where = block_rows.reshape(slots) * col_blocks + block_cols.reshape(slots)
    live = slot < block_count.reshape(())
    hit = (where[:, None] == jnp.arange(places, dtype=jnp.int32)[None, :]) & live[:, None]
    which = jnp.sum(jnp.where(hit, slot[:, None], 0), axis=0)
    kind = 2 + jnp.sum(jnp.where(hit, block_type.reshape(slots)[:, None] - 2, 0), axis=0)
    tab = jnp.stack([which, kind]).astype(jnp.int32)

    vmem, anyspace, smem = pltpu.VMEM, pl.ANY, pltpu.SMEM
    dma = pltpu.SemaphoreType.DMA
    hz, gx = max(H - 1, 1), max(G - 1, 1)
    return pl.pallas_call(
        functools.partial(kernel, n_prow, n_pcol, wide, fc),
        out_shape=(
            jax.ShapeDtypeStruct((own_papers, width), BF16),
            jax.ShapeDtypeStruct((own_authors, width), BF16),
        ),
        in_specs=[pl.BlockSpec(memory_space=smem)]
        + [pl.BlockSpec(memory_space=anyspace)] * 6,
        out_specs=(pl.BlockSpec(memory_space=anyspace), pl.BlockSpec(memory_space=vmem)),
        scratch_shapes=[
            vmem((own_papers, width), BF16),
            vmem((width, width), BF16),
            vmem(w_rel.shape, BF16),
            vmem((width, width), BF16),
            vmem((slots, side, side), BF16),
            vmem((H, 2, own_authors, width), BF16),
            vmem((H, 4 * own_authors, width), BF16),
            vmem((H, n_pcol, own_papers, 4 * own_authors), BF16),
            vmem((2, H, own_authors, papers), BF16),
            vmem((nf, G, 2, own_papers, fc), F32),
            vmem((nf, G, own_papers, fc), BF16),
            vmem((nf, G, own_papers, fc), BF16),
            vmem((nf, G, own_papers, fc), BF16),
            vmem((gx, nf, G, own_papers, fc), BF16),
            vmem((nf, 2, G, own_papers, fc), BF16),
            vmem((own_papers, width), BF16),
            vmem((nf, H, own_authors, fc), BF16),
            vmem((nf, H, own_authors, fc), BF16),
            vmem((nf, H, own_authors, fc), F32),
            vmem((nf, H, own_authors, fc), BF16),
            vmem((nf, H, own_authors, fc), BF16),
            vmem((own_authors, width), F32),
            dma((6,)),
            dma((2, hz, 2)), dma((2, hz, 2)), dma((3, hz, 2)), dma((3, hz, 2)),
            dma((nf,)), dma((nf,)), dma((gx, nf)), dma((gx, nf)), dma((nf,)), dma((nf,)),
            dma((nf, H)), dma((nf, H)), dma((nf, H)), dma((nf, H)),
        ],
        compiler_params=pltpu.CompilerParams(
            collective_id=0, has_side_effects=True, vmem_limit_bytes=60 * 1024 * 1024
        ),
    )(tab, author_x, paper_x, w_self, w_rel, w_two, block_vals.reshape(slots, side, side))


def solution(mesh):
    return jax.shard_map(
        functools.partial(per_device, mesh.shape["prow"], mesh.shape["pcol"]),
        mesh=mesh,
        in_specs=(
            P(("prow", "pcol"), None),
            P(("pcol", "prow"), None),
            P(),
            P(),
            P(),
            P("prow", "pcol", None),
            P("prow", "pcol", None),
            P("prow", "pcol", None),
            P("prow", "pcol"),
            P("prow", "pcol", None, None, None),
        ),
        out_specs=(P(("prow", "pcol"), None), P(("pcol", "prow"), None)),
        check_vma=False,
    )
```

```python
import functools

import jax
import jax.numpy as jnp
from jax import lax
from jax.experimental import pallas as pl
from jax.experimental.pallas import tpu as pltpu
from jax.sharding import PartitionSpec as P

MESH = pl.DeviceIdType.MESH
F32 = jnp.float32
BF16 = jnp.bfloat16


def dot(a, b):
    return jnp.dot(a, b, preferred_element_type=F32)


def kernel(
    n_prow, n_pcol, wide, fc,
    rows_h, cols_h, type_h, count_h, author_h, paper_h, w_self_h, w_rel_h, w_two_h, blocks_h,
    hidden, author_out,
    rows, columns, types, count, tab_v, tab, paper, w_self, w_rel, w_two, blocks,
    x_all, msgs, dense, dense_t, acc,
    pair_out, pair_in, x_out, x_in, h_all,
    y_out, y_in, y_acc, z_out, z_in, out_acc,
    local_sem,
    g_send, g_recv, gy_send, gy_recv,
    pair_s, pair_r, xs, xr, hs, hr,
    ys, yr, zs, zr,
):
    i = lax.axis_index("prow")
    j = lax.axis_index("pcol")
    z, y = i // 2, i % 2
    x, c = j // 2, j % 2
    H, G = n_prow // 2, n_pcol // 2
    own_papers, width = paper.shape
    own_authors = author_h.shape[0]
    side = blocks.shape[1]
    authors = own_authors * n_prow
    papers = own_papers * n_pcol
    pair_authors = 2 * own_authors
    nf, nb = width // fc, width // wide
    per = wide // fc
    y_part = z * 2 + 1 - y
    c_part = x * 2 + 1 - c
    low = z < H // 2

    waits = []

    def send(cond, src, dst, ss, rs, di, dj):
        def desc():
            return pltpu.make_async_remote_copy(
                src_ref=src, dst_ref=dst, send_sem=ss, recv_sem=rs,
                device_id=(di, dj), device_id_type=MESH,
            )

        if cond is None:
            desc().start()
        else:
            @pl.when(cond)
            def _():
                desc().start()
        waits.append((cond, desc))

    def arrive(dst, ss, rs):
        pltpu.make_async_remote_copy(
            src_ref=dst, dst_ref=dst, send_sem=ss, recv_sem=rs,
            device_id=(i, c_part), device_id_type=MESH,
        ).wait_recv()

    barrier = pltpu.get_barrier_semaphore()

    def greet(cond, di, dj):
        def go():
            pl.semaphore_signal(barrier, inc=1, device_id=(di, dj), device_id_type=MESH)

        if cond is None:
            go()
        else:
            pl.when(cond)(go)

    up_z, down_z = z < H - 1, z > 0
    peers = 1 + G + up_z.astype(jnp.int32) + down_z.astype(jnp.int32)
    greet(up_z, i + 2, j)
    greet(down_z, i - 2, j)
    greet(None, y_part, j)
    for d in range(1, G):
        greet(None, i, lax.rem(x + d, G) * 2 + c)
    greet(None, i, c_part)

    loads = [
        pltpu.make_async_copy(src, dst, local_sem.at[n])
        for n, (src, dst) in enumerate(
            (
                (rows_h, rows), (cols_h, columns), (type_h, types), (count_h, count),
                (blocks_h, blocks), (w_rel_h, w_rel), (paper_h, paper), (w_self_h, w_self), (w_two_h, w_two),
                (author_h, x_all.at[z, y]),
            )
        )
    ]
    for load in loads:
        load.start()

    pl.semaphore_wait(barrier, peers)

    parts = g_send.shape[2]
    part_rows = own_authors // parts

    def piece(zz, yy, h):
        return x_all.at[zz, yy, pl.ds(h * part_rows, part_rows), :]

    for h in range(parts):
        mine = author_h.at[pl.ds(h * part_rows, part_rows), :]
        send(up_z, mine, piece(z, y, h), g_send.at[0, 0, h], g_recv.at[0, 0, h], i + 2, j)
        send(down_z, mine, piece(z, y, h), g_send.at[1, 0, h], g_recv.at[1, 0, h], i - 2, j)
        send(None, mine, piece(z, y, h), gy_send.at[2, 0, h], gy_recv.at[2, 0, h], y_part, j)

    row_blocks, col_blocks = papers // side, authors // side
    for load in loads[:4]:
        load.wait()
    place = lax.broadcasted_iota(jnp.int32, (1, tab.shape[1]), 1)
    which = jnp.zeros_like(place)
    sort = jnp.full_like(place, 2)
    for slot in range(blocks.shape[0]):
        live = jnp.where(slot < count[0, 0], 1, 0)
        there = rows[0, slot] * col_blocks + columns[0, slot] + (1 - live) * tab.shape[1]
        here = place == there
        which = jnp.where(here, slot, which)
        sort = jnp.where(here, types[0, slot], sort)
    tab_v[0:1] = which
    tab_v[1:2] = sort
    table_copy = pltpu.make_async_copy(tab_v, tab, local_sem.at[0])
    table_copy.start()
    table_copy.wait()
    loads[4].wait()
    p_step, a_step, pair_step = min(side, own_papers), min(side, own_authors), min(side, pair_authors)

    def densify(first, last):
        for rb in range(first, last):
            for cb in range(col_blocks):
                pos = rb * col_blocks + cb
                slot, kind = tab[0, pos], tab[1, pos]
                block = blocks[slot].astype(F32)
                for t in range(2):
                    part = (block * (kind == t).astype(F32)).astype(BF16)
                    for sub in range(side // p_step):
                        row = rb * side + sub * p_step
                        for lane in range(side // pair_step):
                            col = cb * side + lane * pair_step
                            lo = t * pair_authors + col % pair_authors
                            dense[
                                col // pair_authors, row // own_papers,
                                row % own_papers:row % own_papers + p_step, lo:lo + pair_step,
                            ] = part[sub * p_step:(sub + 1) * p_step, lane * pair_step:(lane + 1) * pair_step]
                flip = (block * (kind < 2).astype(F32)).T.astype(BF16)
                for sub in range(side // a_step):
                    owner = (cb * side + sub * a_step) // own_authors
                    dense_t[owner % 2, owner // 2, :, rb * side:(rb + 1) * side] = flip[sub * a_step:(sub + 1) * a_step]

    def z_arrival(s):
        for h in range(parts):
            for way, near, inside, more, to in (
                (0, z - 1 - s, z - 1 - s >= 0, up_z, i + 2),
                (1, z + 1 + s, z + 1 + s <= H - 1, down_z, i - 2),
            ):
                part = piece(near, y, h)

                @pl.when(inside)
                def _():
                    arrive(part, g_send.at[way, s, h], g_recv.at[way, s, h])

                if s + 1 <= H - 2:
                    send(inside & more, part, part, g_send.at[way, s + 1, h], g_recv.at[way, s + 1, h], to, j)
                send(inside, part, part, gy_send.at[way, s, h], gy_recv.at[way, s, h], y_part, j)

    def messages(zz, n):
        pair = x_all[zz].reshape(pair_authors, width)
        cols = slice(n * wide, (n + 1) * wide)
        for t in range(2):
            msgs[zz, t * pair_authors:(t + 1) * pair_authors, cols] = dot(pair, w_rel[t, :, cols]).astype(BF16)

    def hop_one(zz, n, b, cc, first):
        part = dot(dense[zz, b * 2 + cc], msgs[zz, :, n * wide:(n + 1) * wide])
        for p in range(per):
            value = part[:, p * fc:(p + 1) * fc]
            f = n * per + p
            acc[f, b, cc] = value if first else acc[f, b, cc] + value

    def slab(zz, first):
        for n in range(nb):
            messages(zz, n)
            for b in range(G):
                for cc in range(2):
                    hop_one(zz, n, b, cc, first)

    reach = jnp.minimum(z, H - 1 - z)

    def order(k):
        both = k < 2 * reach
        dist = jnp.where(both, k // 2 + 1, k - reach + 1)
        above = jnp.where(both, k % 2 == 0, low)
        return dist, above.astype(jnp.int32), jnp.where(above, z + dist, z - dist)

    def from_y(k):
        dist, way, near = order(k)
        for h in range(parts):
            arrive(piece(near, 1 - y, h), gy_send.at[way, dist - 1, h], gy_recv.at[way, dist - 1, h])
        return near

    half = row_blocks // 2
    densify(0, half)
    z_arrival(0)
    densify(half, row_blocks)
    for load in loads[5:]:
        load.wait()
    for h in range(parts):
        arrive(piece(z, 1 - y, h), gy_send.at[2, 0, h], gy_recv.at[2, 0, h])
    slab(z, True)
    for n in range(nb):
        cols = slice(n * wide, (n + 1) * wide)
        own = dot(paper[...], w_self[:, cols])
        for p in range(per):
            f = n * per + p
            acc[f, x, c] = acc[f, x, c] + own[:, p * fc:(p + 1) * fc]
    if H > 2:
        z_arrival(1)
    for k in range(H - 2):
        slab(from_y(k), False)
        if k + 2 <= H - 2:
            z_arrival(k + 2)
    last = from_y(H - 2)

    def to_pair(n):
        messages(last, n)
        for b in range(G):
            hop_one(last, n, b, 1 - c, False)
        for p in range(per):
            f = n * per + p
            for b in range(G):
                pair_out[f, b] = acc[f, b, 1 - c].astype(BF16)
            send(None, pair_out.at[f], pair_in.at[f], pair_s.at[f], pair_r.at[f], i, c_part)
        for b in range(G):
            hop_one(last, n, b, c, False)

    def to_x(f):
        arrive(pair_in.at[f], pair_s.at[f], pair_r.at[f])
        for b in range(G):
            total = acc[f, b, c] + pair_in[f, b].astype(F32)
            acc[f, b, c] = total
            x_out[f, b] = total.astype(BF16)
        for d in range(1, G):
            send(None, x_out.at[f], x_in.at[d - 1, f], xs.at[d - 1, f], xr.at[d - 1, f],
                 i, lax.rem(x + d, G) * 2 + c)

    def from_x(f):
        for d in range(1, G):
            arrive(x_in.at[d - 1, f], xs.at[d - 1, f], xr.at[d - 1, f])
        for b in range(G):
            total = acc[f, b, c]
            for d in range(1, G):
                total = total + x_in[d - 1, f, b].astype(F32)
            h_all[f, c, b] = jnp.maximum(total, 0.0).astype(BF16)
        send(None, h_all.at[f, c], h_all.at[f, c], hs.at[f], hr.at[f], i, c_part)
        hidden[:, f * fc:(f + 1) * fc] = h_all[f, c, x]

    def target(k):
        return jnp.where(low, H - 1 - k, k)

    def to_y(f):
        arrive(h_all.at[f, 1 - c], hs.at[f], hr.at[f])
        table = jnp.concatenate(
            [h_all[f, q % 2, q // 2] for q in range(n_pcol)], axis=0
        )
        far = dot(dense_t[1 - y].reshape(H * own_authors, papers), table)
        y_out[f] = far.astype(BF16).reshape(H, own_authors, fc)
        for k in range(H):
            b = target(k)
            send(None, y_out.at[f, b], y_in.at[f, b], ys.at[f, b], yr.at[f, b], y_part, j)
        near = dot(dense_t[y].reshape(H * own_authors, papers), table)
        y_acc[f] = near.reshape(H, own_authors, fc)

    def to_z(f):
        for k in range(H):
            b = target(k)
            arrive(y_in.at[f, b], ys.at[f, b], yr.at[f, b])
            total = y_acc[f, b] + y_in[f, b].astype(F32)
            y_acc[f, b] = total
            z_out[f, b] = total.astype(BF16)
            send(b != z, z_out.at[f, b], z_in.at[f, z], zs.at[f, b], zr.at[f, z], b * 2 + y, j)

    def finish(f):
        for s in range(H):
            @pl.when(z != s)
            def _():
                arrive(z_in.at[f, s], zs.at[f, s], zr.at[f, s])
                y_acc[f, z] = y_acc[f, z] + z_in[f, s].astype(F32)

        total = y_acc[f, z]
        high = total.astype(BF16)
        rest = (total - high.astype(F32)).astype(BF16)
        for n in range(nb):
            cols = slice(n * wide, (n + 1) * wide)
            weight = w_two[f * fc:(f + 1) * fc, cols]
            value = dot(high, weight) + dot(rest, weight)
            out_acc[:, cols] = value if f == 0 else out_acc[:, cols] + value

    for n in range(nb):
        to_pair(n)
        if n > 0:
            for p in range(per):
                to_x((n - 1) * per + p)
    for p in range(per):
        to_x((nb - 1) * per + p)

    for f in range(nf):
        from_x(f)
        to_y(f)
        if f >= 1:
            to_z(f - 1)
        if f >= 4:
            finish(f - 4)
    for f in range(max(nf - 4, 0), nf - 2):
        finish(f)
    to_z(nf - 1)
    for f in range(max(nf - 2, 0), nf):
        finish(f)
    author_out[...] = out_acc[...].astype(BF16)

    for cond, desc in waits:
        if cond is None:
            desc().wait_send()
        else:
            @pl.when(cond)
            def _():
                desc().wait_send()


def write_out(hidden, author_out, hidden_h, author_h, sems):
    stores = [
        pltpu.make_async_copy(src, dst, sems.at[n])
        for n, (src, dst) in enumerate(((hidden, hidden_h), (author_out, author_h)))
    ]
    for store in stores:
        store.start()
    for store in stores:
        store.wait()


def per_device(
    n_prow, n_pcol, paper_x, author_x, w_self, w_rel, w_two,
    block_rows, block_cols, block_type, block_count, block_vals,
):
    slots, side = block_vals.shape[2], block_vals.shape[3]
    own_papers, width = paper_x.shape
    own_authors = author_x.shape[0]
    papers, authors = own_papers * n_pcol, own_authors * n_prow
    col_blocks = authors // side
    places = (papers // side) * col_blocks
    lanes = (places + 127) // 128 * 128
    H, G = n_prow // 2, n_pcol // 2
    wide = 256 if width % 256 == 0 else 128
    fc = 128
    nf = width // fc

    vmem, anyspace, smem = pltpu.VMEM, pl.ANY, pltpu.SMEM
    dma = pltpu.SemaphoreType.DMA
    hz, gx = max(H - 1, 1), max(G - 1, 1)
    results = pl.pallas_call(
        functools.partial(kernel, n_prow, n_pcol, wide, fc),
        out_shape=(vmem((own_papers, width), BF16), vmem((own_authors, width), BF16)),
        in_specs=[pl.BlockSpec(memory_space=pltpu.HBM)] * 10,
        out_specs=(pl.BlockSpec(memory_space=vmem),) * 2,
        scratch_shapes=[
            smem((1, slots), jnp.int32),
            smem((1, slots), jnp.int32),
            smem((1, slots), jnp.int32),
            smem((1, 1), jnp.int32),
            vmem((2, lanes), jnp.int32),
            smem((2, lanes), jnp.int32),
            vmem((own_papers, width), BF16),
            vmem((width, width), BF16),
            vmem(w_rel.shape, BF16),
            vmem((width, width), BF16),
            vmem((slots, side, side), BF16),
            vmem((H, 2, own_authors, width), BF16),
            vmem((H, 4 * own_authors, width), BF16),
            vmem((H, n_pcol, own_papers, 4 * own_authors), BF16),
            vmem((2, H, own_authors, papers), BF16),
            vmem((nf, G, 2, own_papers, fc), F32),
            vmem((nf, G, own_papers, fc), BF16),
            vmem((nf, G, own_papers, fc), BF16),
            vmem((nf, G, own_papers, fc), BF16),
            vmem((gx, nf, G, own_papers, fc), BF16),
            vmem((nf, 2, G, own_papers, fc), BF16),
            vmem((nf, H, own_authors, fc), BF16),
            vmem((nf, H, own_authors, fc), BF16),
            vmem((nf, H, own_authors, fc), F32),
            vmem((nf, H, own_authors, fc), BF16),
            vmem((nf, H, own_authors, fc), BF16),
            vmem((own_authors, width), F32),
            dma((10,)),
            dma((2, hz, 2)), dma((2, hz, 2)), dma((3, hz, 2)), dma((3, hz, 2)),
            dma((nf,)), dma((nf,)), dma((gx, nf)), dma((gx, nf)), dma((nf,)), dma((nf,)),
            dma((nf, H)), dma((nf, H)), dma((nf, H)), dma((nf, H)),
        ],
        compiler_params=pltpu.CompilerParams(
            collective_id=0, has_side_effects=True, vmem_limit_bytes=60 * 1024 * 1024
        ),
    )(
        block_rows.reshape(1, slots), block_cols.reshape(1, slots), block_type.reshape(1, slots), block_count,
        author_x, paper_x, w_self, w_rel, w_two, block_vals.reshape(slots, side, side),
    )
    return pl.pallas_call(
        write_out,
        out_shape=(
            jax.ShapeDtypeStruct((own_papers, width), BF16),
            jax.ShapeDtypeStruct((own_authors, width), BF16),
        ),
        in_specs=[pl.BlockSpec(memory_space=vmem)] * 2,
        out_specs=(pl.BlockSpec(memory_space=anyspace),) * 2,
        scratch_shapes=[dma((2,))],
    )(*[pltpu.with_memory_space_constraint(r, pltpu.VMEM) for r in results])


def solution(mesh):
    return jax.shard_map(
        functools.partial(per_device, mesh.shape["prow"], mesh.shape["pcol"]),
        mesh=mesh,
        in_specs=(
            P(("prow", "pcol"), None),
            P(("pcol", "prow"), None),
            P(),
            P(),
            P(),
            P("prow", "pcol", None),
            P("prow", "pcol", None),
            P("prow", "pcol", None),
            P("prow", "pcol"),
            P("prow", "pcol", None, None, None),
        ),
        out_specs=(P(("prow", "pcol"), None), P(("pcol", "prow"), None)),
        check_vma=False,
    )
```

```python
import functools

import jax
import jax.numpy as jnp
from jax import lax
from jax.experimental import pallas as pl
from jax.experimental.pallas import tpu as pltpu
from jax.sharding import PartitionSpec as P

MESH = pl.DeviceIdType.MESH
F32 = jnp.float32
BF16 = jnp.bfloat16


def dot(a, b):
    return jnp.dot(a, b, preferred_element_type=F32)


def kernel(
    n_prow, n_pcol, wide, fc,
    rows_h, cols_h, type_h, count_h, author_h, paper_h, w_self_h, w_rel_h, w_two_h, blocks_h,
    hidden, author_out,
    rows, columns, types, count, tab_v, tab, paper, w_self, w_rel, w_two, blocks,
    x_all, msgs, dense, dense_t, acc,
    pair_out, pair_in, x_out, x_in, h_all,
    y_out, y_in, y_acc, z_out, z_in, out_acc,
    local_sem,
    g_send, g_recv, gy_send, gy_recv,
    pair_s, pair_r, xs, xr, hs, hr,
    ys, yr, zs, zr,
):
    i = lax.axis_index("prow")
    j = lax.axis_index("pcol")
    z, y = i // 2, i % 2
    x, c = j // 2, j % 2
    H, G = n_prow // 2, n_pcol // 2
    own_papers, width = paper.shape
    own_authors = author_h.shape[0]
    side = blocks.shape[1]
    authors = own_authors * n_prow
    papers = own_papers * n_pcol
    pair_authors = 2 * own_authors
    nf, nb = width // fc, width // wide
    per = wide // fc
    y_part = z * 2 + 1 - y
    c_part = x * 2 + 1 - c
    low = z < H // 2

    waits = []

    def send(cond, src, dst, ss, rs, di, dj):
        def desc():
            return pltpu.make_async_remote_copy(
                src_ref=src, dst_ref=dst, send_sem=ss, recv_sem=rs,
                device_id=(di, dj), device_id_type=MESH,
            )

        if cond is None:
            desc().start()
        else:
            @pl.when(cond)
            def _():
                desc().start()
        waits.append((cond, desc))

    def arrive(dst, ss, rs):
        pltpu.make_async_remote_copy(
            src_ref=dst, dst_ref=dst, send_sem=ss, recv_sem=rs,
            device_id=(i, c_part), device_id_type=MESH,
        ).wait_recv()

    barrier = pltpu.get_barrier_semaphore()

    def greet(cond, di, dj):
        def go():
            pl.semaphore_signal(barrier, inc=1, device_id=(di, dj), device_id_type=MESH)

        if cond is None:
            go()
        else:
            pl.when(cond)(go)

    up_z, down_z = z < H - 1, z > 0
    peers = 1 + G + up_z.astype(jnp.int32) + down_z.astype(jnp.int32)
    greet(up_z, i + 2, j)
    greet(down_z, i - 2, j)
    greet(None, y_part, j)
    for d in range(1, G):
        greet(None, i, lax.rem(x + d, G) * 2 + c)
    greet(None, i, c_part)

    loads = [
        pltpu.make_async_copy(src, dst, local_sem.at[n])
        for n, (src, dst) in enumerate(
            (
                (rows_h, rows), (cols_h, columns), (type_h, types), (count_h, count),
                (blocks_h, blocks), (w_rel_h, w_rel), (paper_h, paper), (w_self_h, w_self), (w_two_h, w_two),
                (author_h, x_all.at[z, y]),
            )
        )
    ]
    for load in loads:
        load.start()

    pl.semaphore_wait(barrier, peers)

    parts = g_send.shape[2]
    part_rows = own_authors // parts

    def piece(zz, yy, h):
        return x_all.at[zz, yy, pl.ds(h * part_rows, part_rows), :]

    for h in range(parts):
        mine = author_h.at[pl.ds(h * part_rows, part_rows), :]
        send(up_z, mine, piece(z, y, h), g_send.at[0, 0, h], g_recv.at[0, 0, h], i + 2, j)
        send(down_z, mine, piece(z, y, h), g_send.at[1, 0, h], g_recv.at[1, 0, h], i - 2, j)
        send(None, mine, piece(z, y, h), gy_send.at[2, 0, h], gy_recv.at[2, 0, h], y_part, j)

    row_blocks, col_blocks = papers // side, authors // side
    for load in loads[:4]:
        load.wait()
    place = lax.broadcasted_iota(jnp.int32, (1, tab.shape[1]), 1)
    which = jnp.zeros_like(place)
    sort = jnp.full_like(place, 2)
    for slot in range(blocks.shape[0]):
        live = jnp.where(slot < count[0, 0], 1, 0)
        there = rows[0, slot] * col_blocks + columns[0, slot] + (1 - live) * tab.shape[1]
        here = place == there
        which = jnp.where(here, slot, which)
        sort = jnp.where(here, types[0, slot], sort)
    tab_v[0:1] = which
    tab_v[1:2] = sort
    table_copy = pltpu.make_async_copy(tab_v, tab, local_sem.at[0])
    table_copy.start()
    table_copy.wait()
    loads[4].wait()
    p_step, a_step, pair_step = min(side, own_papers), min(side, own_authors), min(side, pair_authors)

    def densify(first, last):
        for rb in range(first, last):
            for cb in range(col_blocks):
                pos = rb * col_blocks + cb
                slot, kind = tab[0, pos], tab[1, pos]
                block = blocks[slot].astype(F32)
                for t in range(2):
                    part = (block * (kind == t).astype(F32)).astype(BF16)
                    for sub in range(side // p_step):
                        row = rb * side + sub * p_step
                        for lane in range(side // pair_step):
                            col = cb * side + lane * pair_step
                            lo = t * pair_authors + col % pair_authors
                            dense[
                                col // pair_authors, row // own_papers,
                                row % own_papers:row % own_papers + p_step, lo:lo + pair_step,
                            ] = part[sub * p_step:(sub + 1) * p_step, lane * pair_step:(lane + 1) * pair_step]
                flip = (block * (kind < 2).astype(F32)).T.astype(BF16)
                for sub in range(side // a_step):
                    owner = (cb * side + sub * a_step) // own_authors
                    dense_t[owner % 2, owner // 2, :, rb * side:(rb + 1) * side] = flip[sub * a_step:(sub + 1) * a_step]

    def z_arrival(s):
        for h in range(parts):
            for way, near, inside, more, to in (
                (0, z - 1 - s, z - 1 - s >= 0, up_z, i + 2),
                (1, z + 1 + s, z + 1 + s <= H - 1, down_z, i - 2),
            ):
                part = piece(near, y, h)

                @pl.when(inside)
                def _():
                    arrive(part, g_send.at[way, s, h], g_recv.at[way, s, h])

                if s + 1 <= H - 2:
                    send(inside & more, part, part, g_send.at[way, s + 1, h], g_recv.at[way, s + 1, h], to, j)
                send(inside, part, part, gy_send.at[way, s, h], gy_recv.at[way, s, h], y_part, j)

    def messages(zz, n):
        pair = x_all[zz].reshape(pair_authors, width)
        cols = slice(n * wide, (n + 1) * wide)
        for t in range(2):
            msgs[zz, t * pair_authors:(t + 1) * pair_authors, cols] = dot(pair, w_rel[t, :, cols]).astype(BF16)

    def hop_one(zz, n, b, cc, first):
        part = dot(dense[zz, b * 2 + cc], msgs[zz, :, n * wide:(n + 1) * wide])
        for p in range(per):
            value = part[:, p * fc:(p + 1) * fc]
            f = n * per + p
            acc[f, b, cc] = value if first else acc[f, b, cc] + value

    def slab(zz, first):
        for n in range(nb):
            messages(zz, n)
            for b in range(G):
                for cc in range(2):
                    hop_one(zz, n, b, cc, first)

    reach = jnp.minimum(z, H - 1 - z)

    def order(k):
        both = k < 2 * reach
        dist = jnp.where(both, k // 2 + 1, k - reach + 1)
        above = jnp.where(both, k % 2 == 0, low)
        return dist, above.astype(jnp.int32), jnp.where(above, z + dist, z - dist)

    def from_y(k):
        dist, way, near = order(k)
        for h in range(parts):
            arrive(piece(near, 1 - y, h), gy_send.at[way, dist - 1, h], gy_recv.at[way, dist - 1, h])
        return near

    densify(0, row_blocks)
    z_arrival(0)
    for load in loads[5:]:
        load.wait()
    for h in range(parts):
        arrive(piece(z, 1 - y, h), gy_send.at[2, 0, h], gy_recv.at[2, 0, h])
    slab(z, True)
    for n in range(nb):
        cols = slice(n * wide, (n + 1) * wide)
        own = dot(paper[...], w_self[:, cols])
        for p in range(per):
            f = n * per + p
            acc[f, x, c] = acc[f, x, c] + own[:, p * fc:(p + 1) * fc]
    if H > 2:
        z_arrival(1)
    for k in range(H - 2):
        slab(from_y(k), False)
        if k + 2 <= H - 2:
            z_arrival(k + 2)
    last = from_y(H - 2)

    def to_pair(n):
        messages(last, n)
        for b in range(G):
            hop_one(last, n, b, 1 - c, False)
        for p in range(per):
            f = n * per + p
            for b in range(G):
                pair_out[f, b] = acc[f, b, 1 - c].astype(BF16)
            send(None, pair_out.at[f], pair_in.at[f], pair_s.at[f], pair_r.at[f], i, c_part)
        for b in range(G):
            hop_one(last, n, b, c, False)

    def to_x(f):
        arrive(pair_in.at[f], pair_s.at[f], pair_r.at[f])
        for b in range(G):
            total = acc[f, b, c] + pair_in[f, b].astype(F32)
            acc[f, b, c] = total
            x_out[f, b] = total.astype(BF16)
        for d in range(1, G):
            send(None, x_out.at[f], x_in.at[d - 1, f], xs.at[d - 1, f], xr.at[d - 1, f],
                 i, lax.rem(x + d, G) * 2 + c)

    def from_x(f):
        for d in range(1, G):
            arrive(x_in.at[d - 1, f], xs.at[d - 1, f], xr.at[d - 1, f])
        for b in range(G):
            total = acc[f, b, c]
            for d in range(1, G):
                total = total + x_in[d - 1, f, b].astype(F32)
            h_all[f, c, b] = jnp.maximum(total, 0.0).astype(BF16)
        send(None, h_all.at[f, c], h_all.at[f, c], hs.at[f], hr.at[f], i, c_part)
        hidden[:, f * fc:(f + 1) * fc] = h_all[f, c, x]

    def target(k):
        return jnp.where(low, H - 1 - k, k)

    def to_y(f):
        arrive(h_all.at[f, 1 - c], hs.at[f], hr.at[f])
        table = jnp.concatenate(
            [h_all[f, q % 2, q // 2] for q in range(n_pcol)], axis=0
        )
        far = dot(dense_t[1 - y].reshape(H * own_authors, papers), table)
        y_out[f] = far.astype(BF16).reshape(H, own_authors, fc)
        for k in range(H):
            b = target(k)
            send(None, y_out.at[f, b], y_in.at[f, b], ys.at[f, b], yr.at[f, b], y_part, j)
        near = dot(dense_t[y].reshape(H * own_authors, papers), table)
        y_acc[f] = near.reshape(H, own_authors, fc)

    def to_z(f, k_from, k_to):
        for k in range(k_from, k_to):
            b = target(k)
            arrive(y_in.at[f, b], ys.at[f, b], yr.at[f, b])
            total = y_acc[f, b] + y_in[f, b].astype(F32)
            y_acc[f, b] = total
            z_out[f, b] = total.astype(BF16)
            send(b != z, z_out.at[f, b], z_in.at[f, z], zs.at[f, b], zr.at[f, z], b * 2 + y, j)

    def finish(f):
        for s in range(H):
            @pl.when(z != s)
            def _():
                arrive(z_in.at[f, s], zs.at[f, s], zr.at[f, s])
                y_acc[f, z] = y_acc[f, z] + z_in[f, s].astype(F32)

        total = y_acc[f, z]
        high = total.astype(BF16)
        rest = (total - high.astype(F32)).astype(BF16)
        for n in range(nb):
            cols = slice(n * wide, (n + 1) * wide)
            weight = w_two[f * fc:(f + 1) * fc, cols]
            value = dot(high, weight) + dot(rest, weight)
            out_acc[:, cols] = value if f == 0 else out_acc[:, cols] + value

    for n in range(nb):
        to_pair(n)
        if n > 0:
            for p in range(per):
                to_x((n - 1) * per + p)
    for p in range(per):
        to_x((nb - 1) * per + p)

    half = H // 2
    for f in range(nf):
        from_x(f)
        if f >= 2:
            to_z(f - 2, half, H)
        to_y(f)
        if f >= 1:
            to_z(f - 1, 0, half)
        if f >= 4:
            finish(f - 4)
    done = max(nf - 4, 0)
    if nf > 1:
        to_z(nf - 2, half, H)
    if done < nf - 3:
        finish(done)
        done += 1
    to_z(nf - 1, 0, H)
    for f in range(done, nf):
        finish(f)
    author_out[...] = out_acc[...].astype(BF16)

    for cond, desc in waits:
        if cond is None:
            desc().wait_send()
        else:
            @pl.when(cond)
            def _():
                desc().wait_send()


def write_out(hidden, author_out, hidden_h, author_h, sems):
    stores = [
        pltpu.make_async_copy(src, dst, sems.at[n])
        for n, (src, dst) in enumerate(((hidden, hidden_h), (author_out, author_h)))
    ]
    for store in stores:
        store.start()
    for store in stores:
        store.wait()


def per_device(
    n_prow, n_pcol, paper_x, author_x, w_self, w_rel, w_two,
    block_rows, block_cols, block_type, block_count, block_vals,
):
    slots, side = block_vals.shape[2], block_vals.shape[3]
    own_papers, width = paper_x.shape
    own_authors = author_x.shape[0]
    papers, authors = own_papers * n_pcol, own_authors * n_prow
    col_blocks = authors // side
    places = (papers // side) * col_blocks
    lanes = (places + 127) // 128 * 128
    H, G = n_prow // 2, n_pcol // 2
    wide = 256 if width % 256 == 0 else 128
    fc = 128
    nf = width // fc

    vmem, anyspace, smem = pltpu.VMEM, pl.ANY, pltpu.SMEM
    dma = pltpu.SemaphoreType.DMA
    hz, gx = max(H - 1, 1), max(G - 1, 1)
    results = pl.pallas_call(
        functools.partial(kernel, n_prow, n_pcol, wide, fc),
        out_shape=(vmem((own_papers, width), BF16), vmem((own_authors, width), BF16)),
        in_specs=[pl.BlockSpec(memory_space=pltpu.HBM)] * 10,
        out_specs=(pl.BlockSpec(memory_space=vmem),) * 2,
        scratch_shapes=[
            smem((1, slots), jnp.int32),
            smem((1, slots), jnp.int32),
            smem((1, slots), jnp.int32),
            smem((1, 1), jnp.int32),
            vmem((2, lanes), jnp.int32),
            smem((2, lanes), jnp.int32),
            vmem((own_papers, width), BF16),
            vmem((width, width), BF16),
            vmem(w_rel.shape, BF16),
            vmem((width, width), BF16),
            vmem((slots, side, side), BF16),
            vmem((H, 2, own_authors, width), BF16),
            vmem((H, 4 * own_authors, width), BF16),
            vmem((H, n_pcol, own_papers, 4 * own_authors), BF16),
            vmem((2, H, own_authors, papers), BF16),
            vmem((nf, G, 2, own_papers, fc), F32),
            vmem((nf, G, own_papers, fc), BF16),
            vmem((nf, G, own_papers, fc), BF16),
            vmem((nf, G, own_papers, fc), BF16),
            vmem((gx, nf, G, own_papers, fc), BF16),
            vmem((nf, 2, G, own_papers, fc), BF16),
            vmem((nf, H, own_authors, fc), BF16),
            vmem((nf, H, own_authors, fc), BF16),
            vmem((nf, H, own_authors, fc), F32),
            vmem((nf, H, own_authors, fc), BF16),
            vmem((nf, H, own_authors, fc), BF16),
            vmem((own_authors, width), F32),
            dma((10,)),
            dma((2, hz, 2)), dma((2, hz, 2)), dma((3, hz, 2)), dma((3, hz, 2)),
            dma((nf,)), dma((nf,)), dma((gx, nf)), dma((gx, nf)), dma((nf,)), dma((nf,)),
            dma((nf, H)), dma((nf, H)), dma((nf, H)), dma((nf, H)),
        ],
        compiler_params=pltpu.CompilerParams(
            collective_id=0, has_side_effects=True, vmem_limit_bytes=60 * 1024 * 1024
        ),
    )(
        block_rows.reshape(1, slots), block_cols.reshape(1, slots), block_type.reshape(1, slots), block_count,
        author_x, paper_x, w_self, w_rel, w_two, block_vals.reshape(slots, side, side),
    )
    return pl.pallas_call(
        write_out,
        out_shape=(
            jax.ShapeDtypeStruct((own_papers, width), BF16),
            jax.ShapeDtypeStruct((own_authors, width), BF16),
        ),
        in_specs=[pl.BlockSpec(memory_space=vmem)] * 2,
        out_specs=(pl.BlockSpec(memory_space=anyspace),) * 2,
        scratch_shapes=[dma((2,))],
    )(*[pltpu.with_memory_space_constraint(r, pltpu.VMEM) for r in results])


def solution(mesh):
    return jax.shard_map(
        functools.partial(per_device, mesh.shape["prow"], mesh.shape["pcol"]),
        mesh=mesh,
        in_specs=(
            P(("prow", "pcol"), None),
            P(("pcol", "prow"), None),
            P(),
            P(),
            P(),
            P("prow", "pcol", None),
            P("prow", "pcol", None),
            P("prow", "pcol", None),
            P("prow", "pcol"),
            P("prow", "pcol", None, None, None),
        ),
        out_specs=(P(("prow", "pcol"), None), P(("pcol", "prow"), None)),
        check_vma=False,
    )
```

```python
import functools

import jax
import jax.numpy as jnp
from jax import lax
from jax.experimental import pallas as pl
from jax.experimental.pallas import tpu as pltpu
from jax.sharding import PartitionSpec as P

MESH = pl.DeviceIdType.MESH
F32 = jnp.float32
BF16 = jnp.bfloat16


def dot(a, b):
    return jnp.dot(a, b, preferred_element_type=F32)


def kernel(
    n_prow, n_pcol, wide, fc,
    rows_h, cols_h, type_h, count_h, author_h, paper_h, w_self_h, w_rel_h, w_two_h, blocks_h,
    hidden, author_out,
    rows, columns, types, count, tab_v, tab, paper, w_self, w_rel, w_two, blocks,
    x_all, msgs, dense, dense_t, acc,
    pair_out, pair_in, x_out, x_in, h_all,
    y_out, y_in, y_acc, z_out, z_in, out_acc,
    local_sem,
    g_send, g_recv, gy_send, gy_recv,
    pair_s, pair_r, xs, xr, hs, hr,
    ys, yr, zs, zr,
):
    i = lax.axis_index("prow")
    j = lax.axis_index("pcol")
    z, y = i // 2, i % 2
    x, c = j // 2, j % 2
    H, G = n_prow // 2, n_pcol // 2
    own_papers, width = paper.shape
    own_authors = author_h.shape[0]
    side = blocks.shape[1]
    authors = own_authors * n_prow
    papers = own_papers * n_pcol
    pair_authors = 2 * own_authors
    nf, nb = width // fc, width // wide
    per = wide // fc
    y_part = z * 2 + 1 - y
    c_part = x * 2 + 1 - c
    low = z < H // 2

    waits = []

    def send(cond, src, dst, ss, rs, di, dj):
        def desc():
            return pltpu.make_async_remote_copy(
                src_ref=src, dst_ref=dst, send_sem=ss, recv_sem=rs,
                device_id=(di, dj), device_id_type=MESH,
            )

        if cond is None:
            desc().start()
        else:
            @pl.when(cond)
            def _():
                desc().start()
        waits.append((cond, desc))

    def settle(count):
        for cond, desc in waits[:count]:
            if cond is None:
                desc().wait_send()
            else:
                @pl.when(cond)
                def _():
                    desc().wait_send()
        del waits[:count]

    def arrive(dst, ss, rs):
        pltpu.make_async_remote_copy(
            src_ref=dst, dst_ref=dst, send_sem=ss, recv_sem=rs,
            device_id=(i, c_part), device_id_type=MESH,
        ).wait_recv()

    barrier = pltpu.get_barrier_semaphore()

    def greet(cond, di, dj):
        def go():
            pl.semaphore_signal(barrier, inc=1, device_id=(di, dj), device_id_type=MESH)

        if cond is None:
            go()
        else:
            pl.when(cond)(go)

    up_z, down_z = z < H - 1, z > 0
    peers = 1 + G + up_z.astype(jnp.int32) + down_z.astype(jnp.int32)
    greet(up_z, i + 2, j)
    greet(down_z, i - 2, j)
    greet(None, y_part, j)
    for d in range(1, G):
        greet(None, i, lax.rem(x + d, G) * 2 + c)
    greet(None, i, c_part)

    loads = [
        pltpu.make_async_copy(src, dst, local_sem.at[n])
        for n, (src, dst) in enumerate(
            (
                (rows_h, rows), (cols_h, columns), (type_h, types), (count_h, count),
                (blocks_h, blocks), (w_rel_h, w_rel), (paper_h, paper), (w_self_h, w_self), (w_two_h, w_two),
                (author_h, x_all.at[z, y]),
            )
        )
    ]
    for load in loads:
        load.start()

    pl.semaphore_wait(barrier, peers)

    parts = g_send.shape[2]
    part_rows = own_authors // parts

    def piece(zz, yy, h):
        return x_all.at[zz, yy, pl.ds(h * part_rows, part_rows), :]

    for h in range(parts):
        mine = author_h.at[pl.ds(h * part_rows, part_rows), :]
        send(up_z, mine, piece(z, y, h), g_send.at[0, 0, h], g_recv.at[0, 0, h], i + 2, j)
        send(down_z, mine, piece(z, y, h), g_send.at[1, 0, h], g_recv.at[1, 0, h], i - 2, j)
        send(None, mine, piece(z, y, h), gy_send.at[2, 0, h], gy_recv.at[2, 0, h], y_part, j)

    row_blocks, col_blocks = papers // side, authors // side
    for load in loads[:4]:
        load.wait()
    place = lax.broadcasted_iota(jnp.int32, (1, tab.shape[1]), 1)
    which = jnp.zeros_like(place)
    sort = jnp.full_like(place, 2)
    for slot in range(blocks.shape[0]):
        live = jnp.where(slot < count[0, 0], 1, 0)
        there = rows[0, slot] * col_blocks + columns[0, slot] + (1 - live) * tab.shape[1]
        here = place == there
        which = jnp.where(here, slot, which)
        sort = jnp.where(here, types[0, slot], sort)
    tab_v[0:1] = which
    tab_v[1:2] = sort
    table_copy = pltpu.make_async_copy(tab_v, tab, local_sem.at[0])
    table_copy.start()
    table_copy.wait()
    loads[4].wait()
    p_step, a_step, pair_step = min(side, own_papers), min(side, own_authors), min(side, pair_authors)

    def densify(first, last):
        for rb in range(first, last):
            for cb in range(col_blocks):
                pos = rb * col_blocks + cb
                slot, kind = tab[0, pos], tab[1, pos]
                block = blocks[slot].astype(F32)
                for t in range(2):
                    part = (block * (kind == t).astype(F32)).astype(BF16)
                    for sub in range(side // p_step):
                        row = rb * side + sub * p_step
                        for lane in range(side // pair_step):
                            col = cb * side + lane * pair_step
                            lo = t * pair_authors + col % pair_authors
                            dense[
                                col // pair_authors, row // own_papers,
                                row % own_papers:row % own_papers + p_step, lo:lo + pair_step,
                            ] = part[sub * p_step:(sub + 1) * p_step, lane * pair_step:(lane + 1) * pair_step]
                flip = (block * (kind < 2).astype(F32)).T.astype(BF16)
                for sub in range(side // a_step):
                    owner = (cb * side + sub * a_step) // own_authors
                    for lane in range(side // p_step):
                        row = rb * side + lane * p_step
                        dense_t[
                            row // own_papers, owner % 2, owner // 2, :, row % own_papers:row % own_papers + p_step,
                        ] = flip[sub * a_step:(sub + 1) * a_step, lane * p_step:(lane + 1) * p_step]

    def z_arrival(s):
        for h in range(parts):
            for way, near, inside, more, to in (
                (0, z - 1 - s, z - 1 - s >= 0, up_z, i + 2),
                (1, z + 1 + s, z + 1 + s <= H - 1, down_z, i - 2),
            ):
                part = piece(near, y, h)

                @pl.when(inside)
                def _():
                    arrive(part, g_send.at[way, s, h], g_recv.at[way, s, h])

                if s + 1 <= H - 2:
                    send(inside & more, part, part, g_send.at[way, s + 1, h], g_recv.at[way, s + 1, h], to, j)
                send(inside, part, part, gy_send.at[way, s, h], gy_recv.at[way, s, h], y_part, j)

    def messages(zz, n):
        pair = x_all[zz].reshape(pair_authors, width)
        cols = slice(n * wide, (n + 1) * wide)
        for t in range(2):
            msgs[zz, t * pair_authors:(t + 1) * pair_authors, cols] = dot(pair, w_rel[t, :, cols]).astype(BF16)

    def hop_one(zz, n, b, cc, first):
        part = dot(dense[zz, b * 2 + cc], msgs[zz, :, n * wide:(n + 1) * wide])
        for p in range(per):
            value = part[:, p * fc:(p + 1) * fc]
            f = n * per + p
            acc[f, b, cc] = value if first else acc[f, b, cc] + value

    def slab(zz, first):
        for n in range(nb):
            messages(zz, n)
            for b in range(G):
                for cc in range(2):
                    hop_one(zz, n, b, cc, first)

    reach = jnp.minimum(z, H - 1 - z)

    def order(k):
        both = k < 2 * reach
        dist = jnp.where(both, k // 2 + 1, k - reach + 1)
        above = jnp.where(both, k % 2 == 0, low)
        return dist, above.astype(jnp.int32), jnp.where(above, z + dist, z - dist)

    def from_y(k):
        dist, way, near = order(k)
        for h in range(parts):
            arrive(piece(near, 1 - y, h), gy_send.at[way, dist - 1, h], gy_recv.at[way, dist - 1, h])
        return near

    densify(0, row_blocks)
    z_arrival(0)
    for load in loads[5:]:
        load.wait()
    for h in range(parts):
        arrive(piece(z, 1 - y, h), gy_send.at[2, 0, h], gy_recv.at[2, 0, h])
    slab(z, True)
    for n in range(nb):
        cols = slice(n * wide, (n + 1) * wide)
        own = dot(paper[...], w_self[:, cols])
        for p in range(per):
            f = n * per + p
            acc[f, x, c] = acc[f, x, c] + own[:, p * fc:(p + 1) * fc]
    if H > 2:
        z_arrival(1)
    for k in range(H - 2):
        slab(from_y(k), False)
        if k + 2 <= H - 2:
            z_arrival(k + 2)
    gathered = len(waits)
    last = from_y(H - 2)

    def to_pair(n):
        messages(last, n)
        for b in range(G):
            hop_one(last, n, b, 1 - c, False)
        for p in range(per):
            f = n * per + p
            for b in range(G):
                pair_out[f, b] = acc[f, b, 1 - c].astype(BF16)
            send(None, pair_out.at[f], pair_in.at[f], pair_s.at[f], pair_r.at[f], i, c_part)
        for b in range(G):
            hop_one(last, n, b, c, False)

    def to_x(f):
        arrive(pair_in.at[f], pair_s.at[f], pair_r.at[f])
        for b in range(G):
            total = acc[f, b, c] + pair_in[f, b].astype(F32)
            acc[f, b, c] = total
            x_out[f, b] = total.astype(BF16)
        for d in range(1, G):
            send(None, x_out.at[f], x_in.at[d - 1, f], xs.at[d - 1, f], xr.at[d - 1, f],
                 i, lax.rem(x + d, G) * 2 + c)

    def from_x(f):
        for d in range(1, G):
            arrive(x_in.at[d - 1, f], xs.at[d - 1, f], xr.at[d - 1, f])
        for b in range(G):
            total = acc[f, b, c]
            for d in range(1, G):
                total = total + x_in[d - 1, f, b].astype(F32)
            h_all[f, c, b] = jnp.maximum(total, 0.0).astype(BF16)
        send(None, h_all.at[f, c], h_all.at[f, c], hs.at[f], hr.at[f], i, c_part)
        hidden[:, f * fc:(f + 1) * fc] = h_all[f, c, x]

    def target(k):
        return jnp.where(low, H - 1 - k, k)

    start = jnp.where(low, H - H // 2, 0)
    other = jnp.where(low, 0, H // 2)

    def half_sum(f, yy, at, count, core):
        total = None
        for b in range(G):
            part = dot(
                dense_t[b * 2 + core, yy, pl.ds(at, count)].reshape(count * own_authors, own_papers), h_all[f, core, b]
            )
            total = part if total is None else total + part
        return total.reshape(count, own_authors, fc)

    spans = ((start, H // 2, 0), (other, H - H // 2, H // 2))

    def rows_of(f):
        split = 1
        step = own_authors // split
        return [(p, pl.ds(p * step, step)) for p in range(split)]

    def to_y(f):
        for at, count, _ in spans:
            y_acc[f, pl.ds(at, count)] = half_sum(f, 1 - y, at, count, c)
        arrive(h_all.at[f, 1 - c], hs.at[f], hr.at[f])
        for at, count, k_from in spans:
            far = y_acc[f, pl.ds(at, count)] + half_sum(f, 1 - y, at, count, 1 - c)
            y_out[f, pl.ds(at, count)] = far.astype(BF16)
            for k in range(k_from, k_from + count):
                b = target(k)
                for p, rows in rows_of(f):
                    send(None, y_out.at[f, b, rows], y_in.at[f, b, rows], ys.at[f, b, p], yr.at[f, b, p], y_part, j)
        for at, count, _ in spans:
            y_acc[f, pl.ds(at, count)] = half_sum(f, y, at, count, c) + half_sum(f, y, at, count, 1 - c)

    def to_z(f, k_from, k_to):
        for k in range(k_from, k_to):
            b = target(k)
            for p, rows in rows_of(f):
                arrive(y_in.at[f, b, rows], ys.at[f, b, p], yr.at[f, b, p])
                total = y_acc[f, b, rows] + y_in[f, b, rows].astype(F32)
                y_acc[f, b, rows] = total
                z_out[f, b, rows] = total.astype(BF16)
                send(b != z, z_out.at[f, b, rows], z_in.at[f, z, rows], zs.at[f, b, p], zr.at[f, z, p], b * 2 + y, j)

    def finish(f):
        for s in range(H):
            @pl.when(z != s)
            def _():
                for p, rows in rows_of(f):
                    arrive(z_in.at[f, s, rows], zs.at[f, s, p], zr.at[f, s, p])
                y_acc[f, z] = y_acc[f, z] + z_in[f, s].astype(F32)

        total = y_acc[f, z]
        high = total.astype(BF16)
        rest = (total - high.astype(F32)).astype(BF16)
        for n in range(nb):
            cols = slice(n * wide, (n + 1) * wide)
            weight = w_two[f * fc:(f + 1) * fc, cols]
            value = dot(high, weight) + dot(rest, weight)
            out_acc[:, cols] = value if f == 0 else out_acc[:, cols] + value

    to_pair(0)
    for p in range(per):
        to_x(p)
    for n in range(1, nb):
        to_pair(n)
        if n > 1:
            for p in range(per):
                to_x((n - 1) * per + p)
    for p in range(per):
        to_x((nb - 1) * per + p)

    settle(gathered)
    half = H // 2
    for f in range(nf):
        from_x(f)
        if f == nf - 1:
            sent = len(waits)
        if f >= 2:
            to_z(f - 2, half, H)
        to_y(f)
        if f >= 1:
            to_z(f - 1, 0, half)
        if f >= 4:
            finish(f - 4)
    done = max(nf - 4, 0)
    if nf > 1:
        to_z(nf - 2, half, H)
    if done < nf - 3:
        finish(done)
        done += 1
    to_z(nf - 1, 0, H)
    settle(sent)
    for f in range(done, nf):
        finish(f)
    author_out[...] = out_acc[...].astype(BF16)

    settle(len(waits))


def write_out(hidden, author_out, hidden_h, author_h, sems):
    stores = [
        pltpu.make_async_copy(src, dst, sems.at[n])
        for n, (src, dst) in enumerate(((hidden, hidden_h), (author_out, author_h)))
    ]
    for store in stores:
        store.start()
    for store in stores:
        store.wait()


def per_device(
    n_prow, n_pcol, paper_x, author_x, w_self, w_rel, w_two,
    block_rows, block_cols, block_type, block_count, block_vals,
):
    slots, side = block_vals.shape[2], block_vals.shape[3]
    own_papers, width = paper_x.shape
    own_authors = author_x.shape[0]
    papers, authors = own_papers * n_pcol, own_authors * n_prow
    col_blocks = authors // side
    places = (papers // side) * col_blocks
    lanes = (places + 127) // 128 * 128
    H, G = n_prow // 2, n_pcol // 2
    wide = 256 if width % 256 == 0 else 128
    fc = 128
    nf = width // fc

    vmem, anyspace, smem = pltpu.VMEM, pl.ANY, pltpu.SMEM
    dma = pltpu.SemaphoreType.DMA
    hz, gx = max(H - 1, 1), max(G - 1, 1)
    results = pl.pallas_call(
        functools.partial(kernel, n_prow, n_pcol, wide, fc),
        out_shape=(vmem((own_papers, width), BF16), vmem((own_authors, width), BF16)),
        in_specs=[pl.BlockSpec(memory_space=pltpu.HBM)] * 10,
        out_specs=(pl.BlockSpec(memory_space=vmem),) * 2,
        scratch_shapes=[
            smem((1, slots), jnp.int32),
            smem((1, slots), jnp.int32),
            smem((1, slots), jnp.int32),
            smem((1, 1), jnp.int32),
            vmem((2, lanes), jnp.int32),
            smem((2, lanes), jnp.int32),
            vmem((own_papers, width), BF16),
            vmem((width, width), BF16),
            vmem(w_rel.shape, BF16),
            vmem((width, width), BF16),
            vmem((slots, side, side), BF16),
            vmem((H, 2, own_authors, width), BF16),
            vmem((H, 4 * own_authors, width), BF16),
            vmem((H, n_pcol, own_papers, 4 * own_authors), BF16),
            vmem((n_pcol, 2, H, own_authors, own_papers), BF16),
            vmem((nf, G, 2, own_papers, fc), F32),
            vmem((nf, G, own_papers, fc), BF16),
            vmem((nf, G, own_papers, fc), BF16),
            vmem((nf, G, own_papers, fc), BF16),
            vmem((gx, nf, G, own_papers, fc), BF16),
            vmem((nf, 2, G, own_papers, fc), BF16),
            vmem((nf, H, own_authors, fc), BF16),
            vmem((nf, H, own_authors, fc), BF16),
            vmem((nf, H, own_authors, fc), F32),
            vmem((nf, H, own_authors, fc), BF16),
            vmem((nf, H, own_authors, fc), BF16),
            vmem((own_authors, width), F32),
            dma((10,)),
            dma((2, hz, 2)), dma((2, hz, 2)), dma((3, hz, 2)), dma((3, hz, 2)),
            dma((nf,)), dma((nf,)), dma((gx, nf)), dma((gx, nf)), dma((nf,)), dma((nf,)),
            dma((nf, H, 2)), dma((nf, H, 2)), dma((nf, H, 2)), dma((nf, H, 2)),
        ],
        compiler_params=pltpu.CompilerParams(
            collective_id=0, has_side_effects=True, vmem_limit_bytes=60 * 1024 * 1024
        ),
    )(
        block_rows.reshape(1, slots), block_cols.reshape(1, slots), block_type.reshape(1, slots), block_count,
        author_x, paper_x, w_self, w_rel, w_two, block_vals.reshape(slots, side, side),
    )
    return pl.pallas_call(
        write_out,
        out_shape=(
            jax.ShapeDtypeStruct((own_papers, width), BF16),
            jax.ShapeDtypeStruct((own_authors, width), BF16),
        ),
        in_specs=[pl.BlockSpec(memory_space=vmem)] * 2,
        out_specs=(pl.BlockSpec(memory_space=anyspace),) * 2,
        scratch_shapes=[dma((2,))],
    )(*[pltpu.with_memory_space_constraint(r, pltpu.VMEM) for r in results])


def solution(mesh):
    return jax.shard_map(
        functools.partial(per_device, mesh.shape["prow"], mesh.shape["pcol"]),
        mesh=mesh,
        in_specs=(
            P(("prow", "pcol"), None),
            P(("pcol", "prow"), None),
            P(),
            P(),
            P(),
            P("prow", "pcol", None),
            P("prow", "pcol", None),
            P("prow", "pcol", None),
            P("prow", "pcol"),
            P("prow", "pcol", None, None, None),
        ),
        out_specs=(P(("prow", "pcol"), None), P(("pcol", "prow"), None)),
        check_vma=False,
    )
```

```python
import functools

import jax
import jax.numpy as jnp
from jax import lax
from jax.experimental import pallas as pl
from jax.experimental.pallas import tpu as pltpu
from jax.sharding import PartitionSpec as P

MESH = pl.DeviceIdType.MESH
F32 = jnp.float32
BF16 = jnp.bfloat16


def dot(a, b):
    return jnp.dot(a, b, preferred_element_type=F32)


def kernel(
    n_prow, n_pcol, wide, fc,
    rows_h, cols_h, type_h, count_h, author_h, paper_h, w_self_h, w_rel_h, w_two_h, blocks_h,
    hidden, author_out,
    rows, columns, types, count, tab_v, tab, paper, w_self, w_rel, w_two, blocks,
    x_all, msgs, dense, dense_t, acc,
    pair_out, pair_in, x_out, x_in, h_all,
    y_out, y_in, y_acc, z_out, z_in, out_acc,
    local_sem,
    g_send, g_recv, gy_send, gy_recv,
    pair_s, pair_r, xs, xr, hs, hr,
    ys, yr, zs, zr,
):
    i = lax.axis_index("prow")
    j = lax.axis_index("pcol")
    z, y = i // 2, i % 2
    x, c = j // 2, j % 2
    H, G = n_prow // 2, n_pcol // 2
    own_papers, width = paper.shape
    own_authors = author_h.shape[0]
    side = blocks.shape[1]
    authors = own_authors * n_prow
    papers = own_papers * n_pcol
    pair_authors = 2 * own_authors
    nf, nb = width // fc, width // wide
    per = wide // fc
    y_part = z * 2 + 1 - y
    c_part = x * 2 + 1 - c
    low = z < H // 2

    waits = []

    def send(cond, src, dst, ss, rs, di, dj):
        def desc():
            return pltpu.make_async_remote_copy(
                src_ref=src, dst_ref=dst, send_sem=ss, recv_sem=rs,
                device_id=(di, dj), device_id_type=MESH,
            )

        if cond is None:
            desc().start()
        else:
            @pl.when(cond)
            def _():
                desc().start()
        waits.append((cond, desc))

    def settle(count):
        for cond, desc in waits[:count]:
            if cond is None:
                desc().wait_send()
            else:
                @pl.when(cond)
                def _():
                    desc().wait_send()
        del waits[:count]

    def arrive(dst, ss, rs):
        pltpu.make_async_remote_copy(
            src_ref=dst, dst_ref=dst, send_sem=ss, recv_sem=rs,
            device_id=(i, c_part), device_id_type=MESH,
        ).wait_recv()

    barrier = pltpu.get_barrier_semaphore()

    def greet(cond, di, dj):
        def go():
            pl.semaphore_signal(barrier, inc=1, device_id=(di, dj), device_id_type=MESH)

        if cond is None:
            go()
        else:
            pl.when(cond)(go)

    up_z, down_z = z < H - 1, z > 0
    peers = 1 + G + up_z.astype(jnp.int32) + down_z.astype(jnp.int32)
    greet(up_z, i + 2, j)
    greet(down_z, i - 2, j)
    greet(None, y_part, j)
    for d in range(1, G):
        greet(None, i, lax.rem(x + d, G) * 2 + c)
    greet(None, i, c_part)

    loads = [
        pltpu.make_async_copy(src, dst, local_sem.at[n])
        for n, (src, dst) in enumerate(
            (
                (rows_h, rows), (cols_h, columns), (type_h, types), (count_h, count),
                (blocks_h, blocks), (w_rel_h, w_rel), (paper_h, paper), (w_self_h, w_self), (w_two_h, w_two),
                (author_h, x_all.at[z, y]),
            )
        )
    ]
    for load in loads:
        load.start()

    pl.semaphore_wait(barrier, peers)

    parts = g_send.shape[2]
    part_rows = own_authors // parts

    def piece(zz, yy, h):
        return x_all.at[zz, yy, pl.ds(h * part_rows, part_rows), :]

    for h in range(parts):
        mine = author_h.at[pl.ds(h * part_rows, part_rows), :]
        send(up_z, mine, piece(z, y, h), g_send.at[0, 0, h], g_recv.at[0, 0, h], i + 2, j)
        send(down_z, mine, piece(z, y, h), g_send.at[1, 0, h], g_recv.at[1, 0, h], i - 2, j)
        send(None, mine, piece(z, y, h), gy_send.at[2, 0, h], gy_recv.at[2, 0, h], y_part, j)

    row_blocks, col_blocks = papers // side, authors // side
    for load in loads[:4]:
        load.wait()
    place = lax.broadcasted_iota(jnp.int32, (1, tab.shape[1]), 1)
    which = jnp.zeros_like(place)
    sort = jnp.full_like(place, 2)
    for slot in range(blocks.shape[0]):
        live = jnp.where(slot < count[0, 0], 1, 0)
        there = rows[0, slot] * col_blocks + columns[0, slot] + (1 - live) * tab.shape[1]
        here = place == there
        which = jnp.where(here, slot, which)
        sort = jnp.where(here, types[0, slot], sort)
    tab_v[0:1] = which
    tab_v[1:2] = sort
    table_copy = pltpu.make_async_copy(tab_v, tab, local_sem.at[0])
    table_copy.start()
    table_copy.wait()
    loads[4].wait()
    p_step, a_step, pair_step = min(side, own_papers), min(side, own_authors), min(side, pair_authors)

    def densify(first, last):
        for rb in range(first, last):
            for cb in range(col_blocks):
                pos = rb * col_blocks + cb
                slot, kind = tab[0, pos], tab[1, pos]
                block = blocks[slot].astype(F32)
                for t in range(2):
                    part = (block * (kind == t).astype(F32)).astype(BF16)
                    for sub in range(side // p_step):
                        row = rb * side + sub * p_step
                        for lane in range(side // pair_step):
                            col = cb * side + lane * pair_step
                            lo = t * pair_authors + col % pair_authors
                            dense[
                                col // pair_authors, row // own_papers,
                                row % own_papers:row % own_papers + p_step, lo:lo + pair_step,
                            ] = part[sub * p_step:(sub + 1) * p_step, lane * pair_step:(lane + 1) * pair_step]
                flip = (block * (kind < 2).astype(F32)).T.astype(BF16)
                for sub in range(side // a_step):
                    owner = (cb * side + sub * a_step) // own_authors
                    for lane in range(side // p_step):
                        row = rb * side + lane * p_step
                        dense_t[
                            row // own_papers, owner % 2, owner // 2, :, row % own_papers:row % own_papers + p_step,
                        ] = flip[sub * a_step:(sub + 1) * a_step, lane * p_step:(lane + 1) * p_step]

    def z_arrival(s):
        for h in range(parts):
            for way, near, inside, more, to in (
                (0, z - 1 - s, z - 1 - s >= 0, up_z, i + 2),
                (1, z + 1 + s, z + 1 + s <= H - 1, down_z, i - 2),
            ):
                part = piece(near, y, h)

                @pl.when(inside)
                def _():
                    arrive(part, g_send.at[way, s, h], g_recv.at[way, s, h])

                if s + 1 <= H - 2:
                    send(inside & more, part, part, g_send.at[way, s + 1, h], g_recv.at[way, s + 1, h], to, j)
                send(inside, part, part, gy_send.at[way, s, h], gy_recv.at[way, s, h], y_part, j)

    def messages(zz, n):
        pair = x_all[zz].reshape(pair_authors, width)
        cols = slice(n * wide, (n + 1) * wide)
        for t in range(2):
            msgs[zz, t * pair_authors:(t + 1) * pair_authors, cols] = dot(pair, w_rel[t, :, cols]).astype(BF16)

    def hop_one(zz, n, b, cc, first):
        part = dot(dense[zz, b * 2 + cc], msgs[zz, :, n * wide:(n + 1) * wide])
        for p in range(per):
            value = part[:, p * fc:(p + 1) * fc]
            f = n * per + p
            acc[f, b, cc] = value if first else acc[f, b, cc] + value

    def slab(zz, first):
        for n in range(nb):
            messages(zz, n)
            for b in range(G):
                for cc in range(2):
                    hop_one(zz, n, b, cc, first)

    reach = jnp.minimum(z, H - 1 - z)

    def order(k):
        both = k < 2 * reach
        dist = jnp.where(both, k // 2 + 1, k - reach + 1)
        above = jnp.where(both, k % 2 == 0, low)
        return dist, above.astype(jnp.int32), jnp.where(above, z + dist, z - dist)

    def from_y(k):
        dist, way, near = order(k)
        for h in range(parts):
            arrive(piece(near, 1 - y, h), gy_send.at[way, dist - 1, h], gy_recv.at[way, dist - 1, h])
        return near

    densify(0, row_blocks)
    z_arrival(0)
    for load in loads[5:]:
        load.wait()
    for h in range(parts):
        arrive(piece(z, 1 - y, h), gy_send.at[2, 0, h], gy_recv.at[2, 0, h])
    slab(z, True)
    for n in range(nb):
        cols = slice(n * wide, (n + 1) * wide)
        own = dot(paper[...], w_self[:, cols])
        for p in range(per):
            f = n * per + p
            acc[f, x, c] = acc[f, x, c] + own[:, p * fc:(p + 1) * fc]
    if H > 2:
        z_arrival(1)
    for k in range(H - 2):
        slab(from_y(k), False)
        if k + 2 <= H - 2:
            z_arrival(k + 2)
    gathered = len(waits)
    last = from_y(H - 2)

    def to_pair(n):
        messages(last, n)
        for b in range(G):
            hop_one(last, n, b, 1 - c, False)
        for p in range(per):
            f = n * per + p
            for b in range(G):
                pair_out[f, b] = acc[f, b, 1 - c].astype(BF16)
            send(None, pair_out.at[f], pair_in.at[f], pair_s.at[f], pair_r.at[f], i, c_part)
        for b in range(G):
            hop_one(last, n, b, c, False)

    def to_x(f):
        arrive(pair_in.at[f], pair_s.at[f], pair_r.at[f])
        for b in range(G):
            total = acc[f, b, c] + pair_in[f, b].astype(F32)
            acc[f, b, c] = total
            x_out[f, b] = total.astype(BF16)
        for d in range(1, G):
            send(None, x_out.at[f], x_in.at[d - 1, f], xs.at[d - 1, f], xr.at[d - 1, f],
                 i, lax.rem(x + d, G) * 2 + c)

    def from_x(f):
        for d in range(1, G):
            arrive(x_in.at[d - 1, f], xs.at[d - 1, f], xr.at[d - 1, f])
        for b in range(G):
            total = acc[f, b, c]
            for d in range(1, G):
                total = total + x_in[d - 1, f, b].astype(F32)
            h_all[f, c, b] = jnp.maximum(total, 0.0).astype(BF16)
        send(None, h_all.at[f, c], h_all.at[f, c], hs.at[f], hr.at[f], i, c_part)
        hidden[:, f * fc:(f + 1) * fc] = h_all[f, c, x]

    def target(k):
        return jnp.where(low, H - 1 - k, k)

    start = jnp.where(low, H - H // 2, 0)
    other = jnp.where(low, 0, H // 2)

    def half_sum(f, yy, at, count, core):
        total = None
        for b in range(G):
            part = dot(
                dense_t[b * 2 + core, yy, pl.ds(at, count)].reshape(count * own_authors, own_papers), h_all[f, core, b]
            )
            total = part if total is None else total + part
        return total.reshape(count, own_authors, fc)

    spans = ((start, H // 2, 0), (other, H - H // 2, H // 2))

    def rows_of(f):
        split = 1
        step = own_authors // split
        return [(p, pl.ds(p * step, step)) for p in range(split)]

    def to_y(f):
        for at, count, _ in spans:
            y_acc[f, pl.ds(at, count)] = half_sum(f, 1 - y, at, count, c)
        arrive(h_all.at[f, 1 - c], hs.at[f], hr.at[f])
        for at, count, k_from in spans:
            far = y_acc[f, pl.ds(at, count)] + half_sum(f, 1 - y, at, count, 1 - c)
            y_out[f, pl.ds(at, count)] = far.astype(BF16)
            for k in range(k_from, k_from + count):
                b = target(k)
                for p, rows in rows_of(f):
                    send(None, y_out.at[f, b, rows], y_in.at[f, b, rows], ys.at[f, b, p], yr.at[f, b, p], y_part, j)
        for at, count, _ in spans:
            y_acc[f, pl.ds(at, count)] = half_sum(f, y, at, count, c) + half_sum(f, y, at, count, 1 - c)

    def to_z(f, k_from, k_to):
        for k in range(k_from, k_to):
            b = target(k)
            for p, rows in rows_of(f):
                arrive(y_in.at[f, b, rows], ys.at[f, b, p], yr.at[f, b, p])
                total = y_acc[f, b, rows] + y_in[f, b, rows].astype(F32)
                y_acc[f, b, rows] = total
                z_out[f, b, rows] = total.astype(BF16)
                send(b != z, z_out.at[f, b, rows], z_in.at[f, z, rows], zs.at[f, b, p], zr.at[f, z, p], b * 2 + y, j)

    def finish(f):
        for s in range(H):
            @pl.when(z != s)
            def _():
                for p, rows in rows_of(f):
                    arrive(z_in.at[f, s, rows], zs.at[f, s, p], zr.at[f, s, p])
                y_acc[f, z] = y_acc[f, z] + z_in[f, s].astype(F32)

        total = y_acc[f, z]
        high = total.astype(BF16)
        rest = (total - high.astype(F32)).astype(BF16)
        for n in range(nb):
            cols = slice(n * wide, (n + 1) * wide)
            weight = w_two[f * fc:(f + 1) * fc, cols]
            value = dot(high, weight) + dot(rest, weight)
            out_acc[:, cols] = value if f == 0 else out_acc[:, cols] + value

    to_pair(0)
    for p in range(per):
        to_x(p)
    for n in range(1, nb):
        to_pair(n)
        if n > 1:
            for p in range(per):
                to_x((n - 1) * per + p)
    for p in range(per):
        to_x((nb - 1) * per + p)

    settle(gathered)
    half = H // 2
    for f in range(nf):
        from_x(f)
        if f == nf - 1:
            sent = len(waits)
        if f >= 2:
            to_z(f - 2, half, H)
        to_y(f)
        if f >= 1:
            to_z(f - 1, 0, half)
    done = 0
    if nf > 1:
        to_z(nf - 2, half, H)
    while done < nf - 3:
        finish(done)
        done += 1
    to_z(nf - 1, 0, H)
    settle(sent)
    for f in range(done, nf):
        finish(f)
    author_out[...] = out_acc[...].astype(BF16)

    settle(len(waits))


def write_out(hidden, author_out, hidden_h, author_h, sems):
    stores = [
        pltpu.make_async_copy(src, dst, sems.at[n])
        for n, (src, dst) in enumerate(((hidden, hidden_h), (author_out, author_h)))
    ]
    for store in stores:
        store.start()
    for store in stores:
        store.wait()


def per_device(
    n_prow, n_pcol, paper_x, author_x, w_self, w_rel, w_two,
    block_rows, block_cols, block_type, block_count, block_vals,
):
    slots, side = block_vals.shape[2], block_vals.shape[3]
    own_papers, width = paper_x.shape
    own_authors = author_x.shape[0]
    papers, authors = own_papers * n_pcol, own_authors * n_prow
    col_blocks = authors // side
    places = (papers // side) * col_blocks
    lanes = (places + 127) // 128 * 128
    H, G = n_prow // 2, n_pcol // 2
    wide = 256 if width % 256 == 0 else 128
    fc = 128
    nf = width // fc

    vmem, anyspace, smem = pltpu.VMEM, pl.ANY, pltpu.SMEM
    dma = pltpu.SemaphoreType.DMA
    hz, gx = max(H - 1, 1), max(G - 1, 1)
    results = pl.pallas_call(
        functools.partial(kernel, n_prow, n_pcol, wide, fc),
        out_shape=(vmem((own_papers, width), BF16), vmem((own_authors, width), BF16)),
        in_specs=[pl.BlockSpec(memory_space=pltpu.HBM)] * 10,
        out_specs=(pl.BlockSpec(memory_space=vmem),) * 2,
        scratch_shapes=[
            smem((1, slots), jnp.int32),
            smem((1, slots), jnp.int32),
            smem((1, slots), jnp.int32),
            smem((1, 1), jnp.int32),
            vmem((2, lanes), jnp.int32),
            smem((2, lanes), jnp.int32),
            vmem((own_papers, width), BF16),
            vmem((width, width), BF16),
            vmem(w_rel.shape, BF16),
            vmem((width, width), BF16),
            vmem((slots, side, side), BF16),
            vmem((H, 2, own_authors, width), BF16),
            vmem((H, 4 * own_authors, width), BF16),
            vmem((H, n_pcol, own_papers, 4 * own_authors), BF16),
            vmem((n_pcol, 2, H, own_authors, own_papers), BF16),
            vmem((nf, G, 2, own_papers, fc), F32),
            vmem((nf, G, own_papers, fc), BF16),
            vmem((nf, G, own_papers, fc), BF16),
            vmem((nf, G, own_papers, fc), BF16),
            vmem((gx, nf, G, own_papers, fc), BF16),
            vmem((nf, 2, G, own_papers, fc), BF16),
            vmem((nf, H, own_authors, fc), BF16),
            vmem((nf, H, own_authors, fc), BF16),
            vmem((nf, H, own_authors, fc), F32),
            vmem((nf, H, own_authors, fc), BF16),
            vmem((nf, H, own_authors, fc), BF16),
            vmem((own_authors, width), F32),
            dma((10,)),
            dma((2, hz, 2)), dma((2, hz, 2)), dma((3, hz, 2)), dma((3, hz, 2)),
            dma((nf,)), dma((nf,)), dma((gx, nf)), dma((gx, nf)), dma((nf,)), dma((nf,)),
            dma((nf, H, 2)), dma((nf, H, 2)), dma((nf, H, 2)), dma((nf, H, 2)),
        ],
        compiler_params=pltpu.CompilerParams(
            collective_id=0, has_side_effects=True, vmem_limit_bytes=60 * 1024 * 1024
        ),
    )(
        block_rows.reshape(1, slots), block_cols.reshape(1, slots), block_type.reshape(1, slots), block_count,
        author_x, paper_x, w_self, w_rel, w_two, block_vals.reshape(slots, side, side),
    )
    return pl.pallas_call(
        write_out,
        out_shape=(
            jax.ShapeDtypeStruct((own_papers, width), BF16),
            jax.ShapeDtypeStruct((own_authors, width), BF16),
        ),
        in_specs=[pl.BlockSpec(memory_space=vmem)] * 2,
        out_specs=(pl.BlockSpec(memory_space=anyspace),) * 2,
        scratch_shapes=[dma((2,))],
    )(*[pltpu.with_memory_space_constraint(r, pltpu.VMEM) for r in results])


def solution(mesh):
    return jax.shard_map(
        functools.partial(per_device, mesh.shape["prow"], mesh.shape["pcol"]),
        mesh=mesh,
        in_specs=(
            P(("prow", "pcol"), None),
            P(("pcol", "prow"), None),
            P(),
            P(),
            P(),
            P("prow", "pcol", None),
            P("prow", "pcol", None),
            P("prow", "pcol", None),
            P("prow", "pcol"),
            P("prow", "pcol", None, None, None),
        ),
        out_specs=(P(("prow", "pcol"), None), P(("pcol", "prow"), None)),
        check_vma=False,
    )
```
